512 devices in a mesh: region: 16 (over y, core), var: 32 (over z, x).
Axes of the slice: x: 4, y: 8, z: 8, core: 2. Of those that a mesh axis runs over, the one named last changes fastest.
Arguments:
- state: float32 [262144, 768], P(('region', 'var')), may hold values from -6 to 6
- taper: bfloat16 [4, 262144, 384], P(None, ('region', 'var')), may hold values from 0.19921875 to 1
- block_mask: int32 [4, 2048, 3], P(None, ('region', 'var')), may hold values 0 or 1
- anom_fly: float32 [16, 384, 768], P('region', 'var'), may hold values from -6 to 6
- incr_fly: float32 [16, 384, 768], P('region', 'var'), may hold values from -6 to 6
- anom_new: float32 [3, 384, 768], P(None, 'var'), may hold values from -6 to 6
- incr_new: float32 [3, 384, 768], P(None, 'var'), may hold values from -6 to 6
Outputs:
- updated: float32 [262144, 768], P(('region', 'var'))
The draws below stay inside these ranges and needn't reach their ends.
All inputs are finite; a program needn't handle non-finite values. No bound on the sum of `block_mask` on one device may be relied on, other than what follows from the above.
Results may differ from the reference program's by a relative error of at most 0.0003.
Values sent between devices are 32-bit elements; how exact they have to be, the bound alone decides.
No kernel may reach another device: no remote copies, remote signals or barrier semaphores. Data moves between devices by JAX's collectives and lax.ppermute only.
A program may use at most 64 MiB of HBM per device.

```python
import jax
import jax.numpy as jnp
from jax import lax

MEMBERS = 768
OBS = 384
BLOCK = 128
TICKS = 4
ROWS_DEV = 512
ROWS = 262144
NEWB = 3
N_REGION = 16
N_VAR = 32


def touch_ends(values, stream_key, least, high):
    spot = [jax.random.randint(jax.random.fold_in(stream_key, axis), (), 0, length) for axis, length in enumerate(values.shape)]
    main_axis = values.shape.index(max(values.shape))
    neighbour = spot[:main_axis] + [(spot[main_axis] + 1) % values.shape[main_axis]] + spot[main_axis + 1:]
    return values.at[tuple(spot)].set(least).at[tuple(neighbour)].set(high)


def block_scale(stream_key, dims, pieces, smallest, high):
    factor_of = 1.0
    for axis_at, blocks in pieces:
        draws = jax.random.uniform(jax.random.fold_in(jax.random.fold_in(stream_key, 6), axis_at), (blocks,), jnp.float32, smallest / len(pieces), high / len(pieces))
        factor_of = factor_of * jnp.repeat(jnp.exp(draws), dims[axis_at] // blocks).reshape((-1,) + (1,) * (len(dims) - 1 - axis_at))
    return factor_of


def noise(stream_key, dims, scale, bound, split=(), held_as=jnp.bfloat16):
    entries = scale * jax.random.normal(stream_key, dims, jnp.float32)
    if split:
        entries = entries * block_scale(stream_key, dims, split, -0.22, 0.18)
    return jnp.clip(entries, -bound, bound).astype(held_as)


def setup_inputs(seed: int = 0) -> dict:
    key_list = jax.random.split(jax.random.key(seed), 8)
    state = noise(key_list[0], (ROWS, MEMBERS), 1.0, 6.0, ((0, 512),), jnp.float32)
    taper = jnp.clip(0.19921875 + 0.80078125 * jax.random.uniform(key_list[1], (TICKS, ROWS, OBS), jnp.float32) ** block_scale(key_list[1], (TICKS, ROWS, OBS), ((1, 512),), -0.2, 0.2), 0.19921875, 1.0).astype(jnp.bfloat16)
    block_mask = touch_ends((jax.random.randint(key_list[2], (TICKS, ROWS // BLOCK, OBS // BLOCK), 0, 2) < 1).astype(jnp.int32), jax.random.fold_in(key_list[2], 1), 0, 1)
    anom_fly = noise(key_list[3], (N_REGION, OBS, MEMBERS), 1.0, 6.0, ((0, 16), (1, 32)), jnp.float32)
    incr_fly = noise(key_list[4], (N_REGION, OBS, MEMBERS), 1.0, 6.0, ((0, 16), (1, 32)), jnp.float32)
    anom_new = noise(key_list[5], (NEWB, OBS, MEMBERS), 1.0, 6.0, ((1, 32),), jnp.float32)
    incr_new = noise(key_list[6], (NEWB, OBS, MEMBERS), 1.0, 6.0, ((1, 32),), jnp.float32)
    return dict(state=state, taper=taper, block_mask=block_mask, anom_fly=anom_fly, incr_fly=incr_fly, anom_new=anom_new, incr_new=incr_new)


def reference(state, taper, block_mask, anom_fly, incr_fly, anom_new, incr_new):
    span = N_VAR * ROWS_DEV
    all_anom = jnp.concatenate([anom_fly[::-1], anom_new], 0)
    all_incr = jnp.concatenate([incr_fly[::-1], incr_new], 0)

    def one_region(region_id):
        state_rows = lax.dynamic_slice_in_dim(state, region_id * span, span, 0)
        for tick_num in range(TICKS):
            batch_num = (N_REGION - 1 + tick_num) - region_id
            anomaly = lax.dynamic_index_in_dim(all_anom, batch_num, 0, keepdims=False)
            increment_rows = lax.dynamic_index_in_dim(all_incr, batch_num, 0, keepdims=False)
            local_taper = lax.dynamic_slice_in_dim(taper[tick_num], region_id * span, span, 0).astype(jnp.float32)
            block_flags = lax.dynamic_slice_in_dim(block_mask[tick_num], region_id * (span // BLOCK), span // BLOCK, 0)
            expanded = jnp.repeat(jnp.repeat(block_flags, BLOCK, 0), BLOCK, 1).astype(jnp.float32)
            covar = jnp.dot(state_rows, anomaly.T, precision=lax.Precision.HIGHEST, preferred_element_type=jnp.float32)
            weights = local_taper * expanded * covar / (MEMBERS - 1)
            state_rows = state_rows + jnp.dot(weights, increment_rows, precision=lax.Precision.HIGHEST, preferred_element_type=jnp.float32)
        return state_rows

    regions = lax.map(one_region, jnp.arange(N_REGION, dtype=jnp.int32))
    return regions.reshape(N_REGION * span, MEMBERS)
```

```python
import functools

import jax
import jax.numpy as jnp
from jax import lax
from jax.experimental import pallas as pl
from jax.experimental.pallas import tpu as pltpu
from jax.sharding import PartitionSpec as P

MEMBERS = 768
HALF = 384
OBS = 384
BLOCK = 128
TICKS = 4
ROWS = 512
SHARE = 12
PACK = 24
SLOTS = 512
N_VAR = 32
N_Y = 8
F32 = jnp.float32
BF16 = jnp.bfloat16


def route(move):
    pairs = []
    for y in range(N_Y):
        for core in range(2):
            for z in range(8):
                for x in range(4):
                    to = move(y, core, z, x)
                    if to is not None:
                        ty, tc, tz, tx = to
                        here = (y * 2 + core) * N_VAR + z * 4 + x
                        there = (ty * 2 + tc) * N_VAR + (tz % 8) * 4 + tx % 4
                        pairs.append((here, there))
    return pairs


def send(block, move):
    return lax.ppermute(block, ("region", "var"), route(move))


def flip(y, core, z, x):
    return y, 1 - core, z, x


def up_y(step):
    return lambda y, core, z, x: (y + step, core, z, x) if y + step < N_Y else None


def packed(anom, incr):
    return jnp.concatenate(
        [anom[..., :8, :], incr[..., :8, :], anom[..., 8:, :], incr[..., 8:, :]], axis=-2
    )


def column_half(block, which):
    return lax.dynamic_slice_in_dim(block, which * HALF, HALF, block.ndim - 1)


def chip_shares(core, y, anom_fly, incr_fly, anom_new, incr_new):
    own = packed(anom_fly[0], incr_fly[0])
    mine = column_half(own, core)
    other = send(column_half(own, 1 - core), flip)
    pair = jnp.stack([jnp.where(core == 1, mine, other), jnp.where(core == 1, other, mine)])
    below = send(pair, up_y(1))
    below2 = send(pair[0], up_y(2))
    fresh = column_half(packed(anom_new, incr_new), core)
    return jnp.stack(
        [
            pair[0],
            pair[1],
            jnp.where(y == 0, fresh[0], below[0]),
            jnp.where(y == 0, fresh[1], below[1]),
            jnp.where(y == 0, fresh[2], jnp.where(y == 1, fresh[0], below2)),
        ]
    )


def slot_table(source):
    slot = jnp.arange(SLOTS)
    part, piece, lane = slot // 256, (slot % 256) // 8, slot % 8
    row = jnp.where(part == 0, lane, 8 + lane)
    obs = source(piece) * SHARE + row
    obs = jnp.where((part == 1) & (lane >= 4), -1, obs)
    return (jnp.arange(OBS)[:, None] == obs[None, :]).astype(BF16)


def localize_kernel(mask_ref, taper_ref, table_ref, out_ref):
    tick = pl.program_id(0)
    for rb in range(ROWS // BLOCK):
        rows = pl.ds(rb * BLOCK, BLOCK)
        parts = []
        for ob in range(OBS // BLOCK):
            flag = mask_ref[(tick * (ROWS // BLOCK) + rb) * (OBS // BLOCK) + ob].astype(F32)
            tile = taper_ref[0, rows, pl.ds(ob * BLOCK, BLOCK)].astype(F32)
            parts.append((tile * flag).astype(BF16))
        kept = jnp.concatenate(parts, axis=1)
        out_ref[0, rows, :] = jnp.dot(kept, table_ref[...], preferred_element_type=F32).astype(BF16)


def localizers(taper, block_mask, table):
    return pl.pallas_call(
        localize_kernel,
        out_shape=jax.ShapeDtypeStruct((TICKS, ROWS, SLOTS), BF16),
        grid_spec=pltpu.PrefetchScalarGridSpec(
            num_scalar_prefetch=1,
            grid=(TICKS,),
            in_specs=[
                pl.BlockSpec((1, ROWS, OBS), lambda t, m: (t, 0, 0)),
                pl.BlockSpec((OBS, SLOTS), lambda t, m: (0, 0)),
            ],
            out_specs=pl.BlockSpec((1, ROWS, SLOTS), lambda t, m: (t, 0, 0)),
        ),
        cost_estimate=pl.CostEstimate(flops=8 * ROWS * OBS * SLOTS, bytes_accessed=4 << 20, transcendentals=0),
        name="localize",
    )(block_mask.reshape(-1), taper, table)


def halves(a):
    hi = a.astype(BF16)
    return hi, (a - hi.astype(F32)).astype(BF16)


def dot3(a, b, dims):
    def one(p, q):
        return lax.dot_general(p, q, (dims, ((), ())), preferred_element_type=F32)

    return one(a[0], b[0]) + one(a[0], b[1]) + one(a[1], b[0])


def tick_kernel(where_ref, state_ref, local_ref, own_ref, par_ref, out_ref):
    core = where_ref[0]
    mine = pl.ds(pl.multiple_of(core * HALF, BLOCK), HALF)
    other = pl.ds(pl.multiple_of((1 - core) * HALF, BLOCK), HALF)

    def rows(ref, part):
        tile = ref[:, 0, 8 * part : 8 * part + 8, :] if len(ref.shape) == 4 else ref[:, 8 * part : 8 * part + 8, :]
        return halves(tile.reshape(256, HALF))

    own = [rows(own_ref, part) for part in range(3)]
    par = [rows(par_ref, part) for part in range(3)]
    for rb in range(2):
        here = pl.ds(rb * 256, 256)
        left, right = state_ref[here, mine], state_ref[here, other]
        x_own, x_par = halves(left), halves(right)
        trans = ((1,), (1,))
        plain = ((1,), (0,))
        cross8 = dot3(x_own, own[0], trans) + dot3(x_par, par[0], trans)
        cross4 = dot3(x_own, own[2], trans) + dot3(x_par, par[2], trans)
        scale = 1.0 / (MEMBERS - 1)
        w8 = local_ref[0, here, :256].astype(F32) * cross8 * scale
        w4 = local_ref[0, here, 256:].astype(F32) * cross4 * scale
        w8, w4 = halves(w8), halves(pltpu.roll(w4, 4, 1))
        out_ref[here, mine] = left + (dot3(w8, own[1], plain) + dot3(w4, own[2], plain))
        out_ref[here, other] = right + (dot3(w8, par[1], plain) + dot3(w4, par[2], plain))


def assimilate(tick, core, state, local, own, par):
    return pl.pallas_call(
        tick_kernel,
        out_shape=jax.ShapeDtypeStruct((ROWS, MEMBERS), F32),
        grid_spec=pltpu.PrefetchScalarGridSpec(
            num_scalar_prefetch=1,
            grid=(1,),
            in_specs=[
                pl.BlockSpec((ROWS, MEMBERS), lambda i, w: (0, 0)),
                pl.BlockSpec((1, ROWS, SLOTS), lambda i, w: (tick, 0, 0)),
                pl.BlockSpec((N_VAR, 1, PACK, HALF), lambda i, w: (0, w[1], 0, 0)),
                pl.BlockSpec((N_VAR, PACK, HALF), lambda i, w: (0, 0, 0)),
            ],
            out_specs=pl.BlockSpec((ROWS, MEMBERS), lambda i, w: (0, 0)),
        ),
        cost_estimate=pl.CostEstimate(flops=12 * ROWS * SLOTS * MEMBERS, bytes_accessed=8 << 20, transcendentals=0),
        name="assimilate",
    )(jnp.stack([core, 1 - core + tick]), state, local, own, par)


def on_device(state, taper, block_mask, anom_fly, incr_fly, anom_new, incr_new):
    region = lax.axis_index("region")
    core, y = region % 2, region // 2
    share = chip_shares(core, y, anom_fly, incr_fly, anom_new, incr_new)
    gathered = lax.all_gather(share, "var", axis=0, tiled=False)
    local = localizers(taper, block_mask, slot_table(lambda piece: piece))
    for tick in range(TICKS):
        give = lax.dynamic_index_in_dim(gathered, tick + core, 1, keepdims=False)
        par = send(give, flip)
        state = assimilate(tick, core, state, local, gathered, par)
    return state


def solution(mesh):
    in_specs = (
        P(("region", "var"), None),
        P(None, ("region", "var"), None),
        P(None, ("region", "var"), None),
        P("region", "var", None),
        P("region", "var", None),
        P(None, "var", None),
        P(None, "var", None),
    )
    return jax.shard_map(
        on_device, mesh=mesh, in_specs=in_specs, out_specs=P(("region", "var"), None), check_vma=False
    )
```

```python
import jax
import jax.numpy as jnp
import numpy as np
from jax import lax
from jax.experimental import pallas as pl
from jax.experimental.pallas import tpu as pltpu
from jax.sharding import PartitionSpec as P

MEMBERS = 768
HALF = 384
OBS = 384
BLOCK = 128
TICKS = 4
ROWS = 512
SHARE = 12
PACK = 24
SLOTS = 384
N_VAR = 32
N_Y = 8
F32 = jnp.float32
BF16 = jnp.bfloat16


def route(move):
    pairs = []
    for y in range(N_Y):
        for core in range(2):
            for z in range(8):
                for x in range(4):
                    to = move(y, core, z, x)
                    if to is not None:
                        ty, tc, tz, tx = to
                        here = (y * 2 + core) * N_VAR + z * 4 + x
                        there = (ty * 2 + tc) * N_VAR + (tz % 8) * 4 + tx % 4
                        pairs.append((here, there))
    return pairs


def send(block, move):
    return lax.ppermute(block, ("region", "var"), route(move))


def flip(y, core, z, x):
    return y, 1 - core, z, x


def up_y(step):
    return lambda y, core, z, x: (y + step, core, z, x) if y + step < N_Y else None


def pack_kernel(core_ref, anom_ref, incr_ref, anom_new_ref, incr_new_ref, mine_ref, other_ref, fresh_ref):
    core = core_ref[0]
    for col in range(HALF // BLOCK):
        to = slice(col * BLOCK, (col + 1) * BLOCK)
        for half, out_ref in ((core, mine_ref), (1 - core, other_ref)):
            lane = half * (HALF // BLOCK) + col
            anom = anom_ref[pl.ds(lane, SHARE, stride=MEMBERS // BLOCK), :]
            incr = incr_ref[pl.ds(lane, SHARE, stride=MEMBERS // BLOCK), :]
            out_ref[0:8, to], out_ref[8:16, to] = anom[:8], incr[:8]
            out_ref[16:20, to], out_ref[20:24, to] = anom[8:], incr[8:]
    mine = pl.ds(pl.multiple_of(core * HALF, BLOCK), HALF)
    for batch in range(3):
        fresh_ref[batch, 0:8] = anom_new_ref[batch, 0:8, mine]
        fresh_ref[batch, 8:16] = incr_new_ref[batch, 0:8, mine]
        fresh_ref[batch, 16:20] = anom_new_ref[batch, 8:12, mine]
        fresh_ref[batch, 20:24] = incr_new_ref[batch, 8:12, mine]


def share_kernel(where_ref, pair_ref, below_ref, below2_ref, fresh_ref, out_ref):
    y = where_ref[0]
    out_ref[0:2] = pair_ref[...]
    out_ref[2:4] = jnp.where(y == 0, fresh_ref[0:2], below_ref[...])
    out_ref[4] = jnp.where(y == 0, fresh_ref[2], jnp.where(y == 1, fresh_ref[0], below2_ref[...]))


def pair_kernel(core_ref, mine_ref, other_ref, out_ref):
    out_ref[1 - core_ref[0]] = mine_ref[...]
    out_ref[core_ref[0]] = other_ref[...]


def small_call(kernel, name, out_shape, scalar, *arrays):
    vmem = pl.BlockSpec(memory_space=pltpu.VMEM)
    many = isinstance(out_shape[0], tuple)
    shapes = tuple(jax.ShapeDtypeStruct(o, F32) for o in (out_shape if many else (out_shape,)))
    return pl.pallas_call(
        kernel,
        out_shape=shapes if many else shapes[0],
        in_specs=[pl.BlockSpec(memory_space=pltpu.SMEM)] + [vmem] * len(arrays),
        out_specs=(vmem,) * len(shapes) if many else vmem,
        name=name,
    )(scalar.reshape(1), *arrays)


def chip_shares(core, y, anom_fly, incr_fly, anom_new, incr_new):
    flat = (SHARE * MEMBERS // BLOCK, BLOCK)
    tile = (PACK, HALF)
    mine, give, fresh = small_call(
        pack_kernel, "pack", (tile, tile, (3, *tile)), core,
        anom_fly.reshape(flat), incr_fly.reshape(flat), anom_new, incr_new,
    )
    other = send(give, flip)
    pair = small_call(pair_kernel, "pair", (2, *tile), core, mine, other)
    below = send(pair, up_y(1))
    below2 = send(pair[0], up_y(2))
    return small_call(share_kernel, "share", (5, *tile), y, pair, below, below2, fresh)


FAR_Z = (0, 1, -1, 2, -2, 3, -3, 4)
FAR_X = (0, 1, -1, 2)


def piece_order():
    first = [(dz, dx) for dz in (0, 4, 1, -1, 2, -2, 3, -3) for dx in FAR_X]
    second = []
    for dx, part in ((0, 0), (0, 1), (1, 0), (-1, 0), (1, 1), (-1, 1), (2, 0), (2, 1)):
        second += [(dz, dx) for dz in FAR_Z[4 * part : 4 * part + 4]]
    return first, second


ORDER = piece_order()
PARTNER = tuple(tuple(ORDER[1 - core].index(piece) for piece in ORDER[core]) for core in range(2))


def both(to_first, to_second):
    def move(y, core, z, x):
        way = (to_first, to_second)[core]
        return None if way is None else (y, core, z + way[0], x + way[1])

    return move


def hold(value, *others):
    return lax.optimization_barrier((value, *others))[0]


def gather_pieces(core, share, local):
    first = core == 0
    up, down = both((1, 0), (0, 1)), both((-1, 0), (0, -1))
    near_up, near_down = both((0, 1), (1, 0)), both((0, -1), (-1, 0))
    to_second = lambda y, core, z, x: (y, 1, z, x) if core == 0 else None
    to_first = lambda y, core, z, x: (y, 0, z, x) if core == 1 else None
    n1 = send(share, near_up)
    n2 = send(share, near_down)
    n3 = send(n1, near_up)
    low = jnp.stack([share, n1, n2, n3])
    up1 = send(low, up)
    down1 = send(low, down)
    only_up, only_down = both(None, (1, 0)), both(None, (-1, 0))
    n4 = send(n2, only_down)
    n5 = send(n3, only_up)
    n6 = send(n4, only_down)
    n7 = send(n5, only_up)
    high = jnp.stack([n4, n5, n6, n7])
    up2 = send(hold(jnp.where(first, up1, high), local), up)
    down2 = send(jnp.where(first, down1, high), down)
    up3 = send(jnp.where(first, up2, up1), up)
    down3 = send(down2, down)
    par_low, par_up1, par_down1 = (send(hold(block, up2), flip) for block in (low, up1, down1))
    par_high = send(hold(high, up2), to_first)
    far_up = send(up3[:2], both((1, 0), None))
    far_down = send(down3[2:], both((-1, 0), None))
    par_up2, par_down2 = send(hold(up2, up3), flip), send(hold(down2, up3), flip)
    par_up3, par_down3 = send(hold(up3, down3), flip), send(down3, flip)
    par_far_up, par_far_down = send(far_up, to_second), send(far_down, to_second)
    own = [low, up1, down1, up2, down2, up3, down3, far_up, far_down, high]
    par = [par_low, par_up1, par_down1, par_up2, par_down2, par_up3, par_down3, par_far_up, par_far_down, par_high]
    return own, par


def slot_table(core, z, x):
    far = jnp.asarray(np.array(ORDER, np.int32))[core]
    source = ((z - far[:, 0]) % 8) * 4 + (x - far[:, 1]) % 4
    lane = jnp.arange(SHARE)
    rows = source[:, None] * SHARE + lane[None, :]
    obs = jnp.concatenate([rows[:, :8].reshape(-1), rows[:, 8:].reshape(-1)])
    return (jnp.arange(OBS)[:, None] == obs[None, :]).astype(BF16)


def localize_kernel(mask_ref, taper_ref, table_ref, out_ref):
    tick = pl.program_id(0)
    for rb in range(ROWS // BLOCK):
        rows = pl.ds(rb * BLOCK, BLOCK)
        parts = []
        for ob in range(OBS // BLOCK):
            flag = mask_ref[(tick * (ROWS // BLOCK) + rb) * (OBS // BLOCK) + ob].astype(F32)
            tile = taper_ref[0, rows, pl.ds(ob * BLOCK, BLOCK)].astype(F32)
            parts.append((tile * flag).astype(BF16))
        kept = jnp.concatenate(parts, axis=1)
        out_ref[0, rows, :] = jnp.dot(kept, table_ref[...], preferred_element_type=F32).astype(BF16)


def localizers(taper, block_mask, table):
    return pl.pallas_call(
        localize_kernel,
        out_shape=jax.ShapeDtypeStruct((TICKS, ROWS, SLOTS), BF16),
        grid_spec=pltpu.PrefetchScalarGridSpec(
            num_scalar_prefetch=1,
            grid=(TICKS,),
            in_specs=[
                pl.BlockSpec((1, ROWS, OBS), lambda t, m: (t, 0, 0)),
                pl.BlockSpec((OBS, SLOTS), lambda t, m: (0, 0)),
            ],
            out_specs=pl.BlockSpec((1, ROWS, SLOTS), lambda t, m: (t, 0, 0)),
        ),
        cost_estimate=pl.CostEstimate(flops=8 * ROWS * OBS * SLOTS, bytes_accessed=4 << 20, transcendentals=0),
        name="localize",
    )(block_mask.reshape(-1), taper, table)


def halves(a):
    hi = a.astype(BF16)
    return hi, (a - hi.astype(F32)).astype(BF16)


def dot3(a, b, dims):
    def one(p, q):
        return lax.dot_general(p, q, (dims, ((), ())), preferred_element_type=F32)

    return one(a[0], b[0]) + one(a[0], b[1]) + one(a[1], b[0])


def ticks_kernel(where_ref, state_ref, local_ref, *refs):
    own_refs, par_refs, out_ref, own_rows, par_rows = refs[:10], refs[10:20], refs[20], refs[21:25], refs[25:29]
    core = where_ref[0]
    mine = pl.ds(pl.multiple_of(core * HALF, BLOCK), HALF)
    other = pl.ds(pl.multiple_of((1 - core) * HALF, BLOCK), HALF)

    @pl.when(pl.program_id(0) == 0)
    def _():
        out_ref[...] = state_ref[...]

    def piece(held, at, of_first):
        array, part = at // 4, at % 4
        if array == 1 and of_first:
            return held[7 + part // 2][part % 2, 0]
        return held[9 if array == 1 else max(array - 1, 0)][part, 0]

    def put(rows, at, anom, incr):
        for (hi, lo), value in ((rows[:2], anom), (rows[2:], incr)):
            hi[at : at + 16], lo[at : at + 16] = halves(value)

    upper = lax.broadcasted_iota(jnp.int32, (8, HALF), 0) < 4

    def arrange(rows, pieces):
        for at in range(0, N_VAR, 4):
            four = pieces(at)
            for k in (0, 2):
                pair = four[k : k + 2]
                put(
                    rows,
                    8 * (at + k),
                    jnp.concatenate([p[0:8] for p in pair], axis=0),
                    jnp.concatenate([p[8:16] for p in pair], axis=0),
                )
            rest = [p[16:24] for p in four]
            turned = [pltpu.roll(p, 4, 0) for p in rest]
            put(
                rows,
                256 + 4 * at,
                jnp.concatenate([jnp.where(upper, rest[k], turned[k + 1]) for k in (0, 2)], axis=0),
                jnp.concatenate([jnp.where(upper, turned[k], rest[k + 1]) for k in (0, 2)], axis=0),
            )

    for me in range(2):

        @pl.when(core == me)
        def _(me=me):
            arrange(own_rows, lambda at: [piece(own_refs, at + k, me == 0) for k in range(4)])
            arrange(par_rows, lambda at: [piece(par_refs, PARTNER[me][at + k], me == 1) for k in range(4)])

    def both_parts(rows, first):
        return rows[first][...], rows[first + 1][...]

    trans, plain = ((1,), (1,)), ((1,), (0,))
    left, right = out_ref[:, mine], out_ref[:, other]
    cross = dot3(halves(left), both_parts(own_rows, 0), trans) + dot3(halves(right), both_parts(par_rows, 0), trans)
    weight = halves(local_ref[0].astype(F32) * cross * (1.0 / (MEMBERS - 1)))
    out_ref[:, mine] = left + dot3(weight, both_parts(own_rows, 2), plain)
    out_ref[:, other] = right + dot3(weight, both_parts(par_rows, 2), plain)


def run_ticks(core, state, local, own, par):
    four, two = (
        pl.BlockSpec((n, 1, PACK, HALF), lambda t, w: (0, 1 - w[0] + t, 0, 0)) for n in (4, 2)
    )
    return pl.pallas_call(
        ticks_kernel,
        out_shape=jax.ShapeDtypeStruct((ROWS, MEMBERS), F32),
        grid_spec=pltpu.PrefetchScalarGridSpec(
            num_scalar_prefetch=1,
            grid=(TICKS,),
            in_specs=[
                pl.BlockSpec((ROWS, MEMBERS), lambda t, w: (0, 0)),
                pl.BlockSpec((1, ROWS, SLOTS), lambda t, w: (t, 0, 0)),
            ]
            + ([four] * 7 + [two] * 2 + [four]) * 2,
            out_specs=pl.BlockSpec((ROWS, MEMBERS), lambda t, w: (0, 0)),
            scratch_shapes=[pltpu.VMEM((OBS, HALF), BF16)] * 8,
        ),
        cost_estimate=pl.CostEstimate(flops=48 * ROWS * SLOTS * MEMBERS, bytes_accessed=16 << 20, transcendentals=0),
        name="ticks",
    )(core.reshape(1), state, local, *own, *par)


def on_device(state, taper, block_mask, anom_fly, incr_fly, anom_new, incr_new):
    region, place = lax.axis_index("region"), lax.axis_index("var")
    core, y = region % 2, region // 2
    share = chip_shares(core, y, anom_fly, incr_fly, anom_new, incr_new)
    local = localizers(taper, block_mask, slot_table(core, place // 4, place % 4))
    own, par = gather_pieces(core, share, local)
    return run_ticks(core, state, local, own, par)


def solution(mesh):
    in_specs = (
        P(("region", "var"), None),
        P(None, ("region", "var"), None),
        P(None, ("region", "var"), None),
        P("region", "var", None),
        P("region", "var", None),
        P(None, "var", None),
        P(None, "var", None),
    )
    return jax.shard_map(
        on_device, mesh=mesh, in_specs=in_specs, out_specs=P(("region", "var"), None), check_vma=False
    )
```

```python
import jax
import jax.numpy as jnp
import numpy as np
from jax import lax
from jax.experimental import pallas as pl
from jax.experimental.pallas import tpu as pltpu
from jax.sharding import PartitionSpec as P


MEMBERS = 768
HALF = 384
OBS = 384
BLOCK = 128
TICKS = 4
ROWS = 512
SHARE = 12
PACK = 24
SLOTS = 384
N_VAR = 32
N_Y = 8
F32 = jnp.float32
BF16 = jnp.bfloat16


def route(move):
    pairs = []
    for y in range(N_Y):
        for core in range(2):
            for z in range(8):
                for x in range(4):
                    to = move(y, core, z, x)
                    if to is not None:
                        ty, tc, tz, tx = to
                        here = (y * 2 + core) * N_VAR + z * 4 + x
                        there = (ty * 2 + tc) * N_VAR + (tz % 8) * 4 + tx % 4
                        pairs.append((here, there))
    return pairs


def send(block, move):
    return lax.ppermute(block, ("region", "var"), route(move))


def flip(y, core, z, x):
    return y, 1 - core, z, x


def up_y(step):
    return lambda y, core, z, x: (y + step, core, z, x) if y + step < N_Y else None


def pack_kernel(core_ref, *refs):
    core = core_ref[0]
    mine_ref, other_ref, fresh_ref = refs[4:7]
    copies = [pltpu.make_async_copy(refs[i], refs[7 + i], refs[11].at[i]) for i in range(4)]
    for copy in copies:
        copy.start()
    for copy in copies:
        copy.wait()
    anom_ref, incr_ref, anom_new_ref, incr_new_ref = refs[7:11]
    for col in range(HALF // BLOCK):
        to = slice(col * BLOCK, (col + 1) * BLOCK)
        for half, out_ref in ((core, mine_ref), (1 - core, other_ref)):
            lane = half * (HALF // BLOCK) + col
            anom = anom_ref[pl.ds(lane, SHARE, stride=MEMBERS // BLOCK), :]
            incr = incr_ref[pl.ds(lane, SHARE, stride=MEMBERS // BLOCK), :]
            out_ref[0:8, to], out_ref[8:16, to] = anom[:8], incr[:8]
            out_ref[16:20, to], out_ref[20:24, to] = anom[8:], incr[8:]
    mine = pl.ds(pl.multiple_of(core * HALF, BLOCK), HALF)
    for batch in range(3):
        fresh_ref[batch, 0:8] = anom_new_ref[batch, 0:8, mine]
        fresh_ref[batch, 8:16] = incr_new_ref[batch, 0:8, mine]
        fresh_ref[batch, 16:20] = anom_new_ref[batch, 8:12, mine]
        fresh_ref[batch, 20:24] = incr_new_ref[batch, 8:12, mine]


def chip_shares(core, y, anom_fly, incr_fly, anom_new, incr_new):
    flat = (SHARE * MEMBERS // BLOCK, BLOCK)
    tile = (PACK, HALF)
    vmem = pl.BlockSpec(memory_space=pltpu.VMEM)
    mine, give, fresh = pl.pallas_call(
        pack_kernel,
        out_shape=tuple(jax.ShapeDtypeStruct(o, F32) for o in (tile, tile, (3, *tile))),
        in_specs=[pl.BlockSpec(memory_space=pltpu.SMEM)] + [pl.BlockSpec(memory_space=pltpu.HBM)] * 4,
        out_specs=(vmem, vmem, vmem),
        scratch_shapes=[pltpu.VMEM(flat, F32)] * 2
        + [pltpu.VMEM((3, SHARE, MEMBERS), F32)] * 2
        + [pltpu.SemaphoreType.DMA((4,))],
        compiler_params=pltpu.CompilerParams(vmem_limit_bytes=4 << 20),
        name="pack",
    )(
        core.reshape(1),
        *(pltpu.with_memory_space_constraint(a, pltpu.HBM) for a in (anom_fly.reshape(flat), incr_fly.reshape(flat), anom_new, incr_new)),
    )
    other = send(give, flip)
    pair = jnp.stack([jnp.where(core == 1, mine, other), jnp.where(core == 1, other, mine)])
    below = send(pair, up_y(1))
    below2 = send(pair[0], up_y(2))
    return jnp.stack(
        [
            pair[0],
            pair[1],
            jnp.where(y == 0, fresh[0], below[0]),
            jnp.where(y == 0, fresh[1], below[1]),
            jnp.where(y == 0, fresh[2], jnp.where(y == 1, fresh[0], below2)),
        ]
    )


FAR_Z = (0, 1, -1, 2, -2, 3, -3, 4)
FAR_X = (0, 1, -1, 2)


def piece_order():
    first = [(dz, dx) for dz in (0, 4, 1, -1, 2, -2, 3, -3) for dx in FAR_X]
    second = []
    for dx, part in ((0, 0), (0, 1), (1, 0), (-1, 0), (1, 1), (-1, 1), (2, 0), (2, 1)):
        second += [(dz, dx) for dz in FAR_Z[4 * part : 4 * part + 4]]
    return first, second


ORDER = piece_order()
PARTNER = tuple(tuple(ORDER[1 - core].index(piece) for piece in ORDER[core]) for core in range(2))


def both(to_first, to_second):
    def move(y, core, z, x):
        way = (to_first, to_second)[core]
        return None if way is None else (y, core, z + way[0], x + way[1])

    return move


def gather_pieces(core, share, make_local):
    first = core == 0
    up, down = both((1, 0), (0, 1)), both((-1, 0), (0, -1))
    near_up, near_down = both((0, 1), (1, 0)), both((0, -1), (-1, 0))
    to_second = lambda y, core, z, x: (y, 1, z, x) if core == 0 else None
    to_first = lambda y, core, z, x: (y, 0, z, x) if core == 1 else None
    only_up, only_down = both(None, (1, 0)), both(None, (-1, 0))
    n1 = send(share, near_up)
    n3 = send(share, both((0, 2), (2, 0)))
    n2 = send(share, near_down)
    low = jnp.stack([share, n1, n2, n3])
    up1 = send(low, up)
    down1 = send(low, down)
    n4 = send(n2, only_down)
    n5 = send(n3, only_up)
    n6 = send(n4, only_down)
    n7 = send(n5, only_up)
    high = jnp.stack([n4, n5, n6, n7])
    up2 = send(jnp.where(first, up1, high), up)
    down2 = send(jnp.where(first, down1, high), down)
    par_low = send(low, flip)
    par_up1 = send(up1, flip)
    par_down1 = send(down1, flip)
    local = make_local(high)
    up3 = send(jnp.where(first, up2, up1), up)
    down3 = send(down2, down)
    par_high = send(high, to_first)
    par_up2 = send(up2, flip)
    par_down2 = send(down2, flip)
    far_up = send(up3[:2], both((1, 0), None))
    far_down = send(down3[2:], both((-1, 0), None))
    par_up3 = send(up3, flip)
    par_down3 = send(down3, flip)
    par_far_up = send(far_up, to_second)
    par_far_down = send(far_down, to_second)
    own = [low, up1, down1, up2, down2, up3, down3, far_up, far_down, high]
    par = [par_low, par_up1, par_down1, par_up2, par_down2, par_up3, par_down3, par_far_up, par_far_down, par_high]
    return own, par, local


def slot_table(core, z, x):
    far = jnp.asarray(np.array(ORDER, np.int32))[core]
    source = ((z - far[:, 0]) % 8) * 4 + (x - far[:, 1]) % 4
    lane = jnp.arange(SHARE)
    rows = source[:, None] * SHARE + lane[None, :]
    obs = jnp.concatenate([rows[:, :8].reshape(-1), rows[:, 8:].reshape(-1)])
    return (jnp.arange(OBS)[:, None] == obs[None, :]).astype(BF16)


def localize_kernel(mask_ref, taper_ref, table_ref, out_ref):
    tick = pl.program_id(0)
    for rb in range(ROWS // BLOCK):
        rows = pl.ds(rb * BLOCK, BLOCK)
        parts = []
        for ob in range(OBS // BLOCK):
            flag = mask_ref[(tick * (ROWS // BLOCK) + rb) * (OBS // BLOCK) + ob].astype(F32).astype(BF16)
            tile = taper_ref[0, rows, pl.ds(ob * BLOCK, BLOCK)]
            parts.append(tile * flag)
        kept = jnp.concatenate(parts, axis=1)
        out_ref[0, rows, :] = jnp.dot(kept, table_ref[...], preferred_element_type=F32).astype(BF16)


def localizers(taper, block_mask, table):
    return pl.pallas_call(
        localize_kernel,
        out_shape=jax.ShapeDtypeStruct((TICKS, ROWS, SLOTS), BF16),
        grid_spec=pltpu.PrefetchScalarGridSpec(
            num_scalar_prefetch=1,
            grid=(TICKS,),
            in_specs=[
                pl.BlockSpec((1, ROWS, OBS), lambda t, m: (t, 0, 0)),
                pl.BlockSpec((OBS, SLOTS), lambda t, m: (0, 0)),
            ],
            out_specs=pl.BlockSpec((1, ROWS, SLOTS), lambda t, m: (t, 0, 0)),
        ),
        cost_estimate=pl.CostEstimate(flops=8 * ROWS * OBS * SLOTS, bytes_accessed=4 << 20, transcendentals=0),
        compiler_params=pltpu.CompilerParams(vmem_limit_bytes=8 << 20),
        name="localize",
    )(block_mask.reshape(-1), taper, table)


def halves(a):
    hi = a.astype(BF16)
    return hi, (a - hi.astype(F32)).astype(BF16)


def ticks_kernel(where_ref, state_ref, local_ref, *refs):
    own_refs, par_refs, out_ref, y_rows, d_rows = refs[:10], refs[10:20], refs[20], refs[21], refs[22]
    core = where_ref[0]

    @pl.when(pl.program_id(0) == 0)
    def _():
        out_ref[...] = state_ref[...]

    def piece(held, at, of_first):
        array, part = at // 4, at % 4
        if array == 1 and of_first:
            return held[7 + part // 2][part % 2, 0]
        return held[9 if array == 1 else max(array - 1, 0)][part, 0]

    def put(columns, at, anom, incr):
        hi, lo = halves(anom)
        for part, value in enumerate((hi, lo, hi)):
            y_rows[at : at + 16, part * MEMBERS + columns : part * MEMBERS + columns + HALF] = value
        hi, lo = halves(incr)
        for part, value in enumerate((hi, lo, hi)):
            d_rows[part * OBS + at : part * OBS + at + 16, columns : columns + HALF] = value

    upper = lax.broadcasted_iota(jnp.int32, (8, HALF), 0) < 4

    def arrange(rows, pieces):
        for at in range(0, N_VAR, 4):
            four = pieces(at)
            for k in (0, 2):
                pair = four[k : k + 2]
                put(
                    rows,
                    8 * (at + k),
                    jnp.concatenate([p[0:8] for p in pair], axis=0),
                    jnp.concatenate([p[8:16] for p in pair], axis=0),
                )
            rest = [p[16:24] for p in four]
            turned = [pltpu.roll(p, 4, 0) for p in rest]
            put(
                rows,
                256 + 4 * at,
                jnp.concatenate([jnp.where(upper, rest[k], turned[k + 1]) for k in (0, 2)], axis=0),
                jnp.concatenate([jnp.where(upper, turned[k], rest[k + 1]) for k in (0, 2)], axis=0),
            )

    for me in range(2):

        @pl.when(core == me)
        def _(me=me):
            arrange(me * HALF, lambda at: [piece(own_refs, at + k, me == 0) for k in range(4)])
            arrange((1 - me) * HALF, lambda at: [piece(par_refs, PARTNER[me][at + k], me == 1) for k in range(4)])

    def product(a, b, dims):
        hi, lo = halves(a)
        return lax.dot_general(
            jnp.concatenate([hi, hi, lo], axis=1), b[...], (dims, ((), ())), preferred_element_type=F32
        )

    cross = product(out_ref[...], y_rows, ((1,), (1,)))
    weight = local_ref[0].astype(F32) * cross * (1.0 / (MEMBERS - 1))
    out_ref[...] += product(weight, d_rows, ((1,), (0,)))


def run_ticks(core, state, local, own, par):
    four, two = (
        pl.BlockSpec((n, 1, PACK, HALF), lambda t, w: (0, 1 - w[0] + t, 0, 0)) for n in (4, 2)
    )
    return pl.pallas_call(
        ticks_kernel,
        out_shape=jax.ShapeDtypeStruct((ROWS, MEMBERS), F32),
        grid_spec=pltpu.PrefetchScalarGridSpec(
            num_scalar_prefetch=1,
            grid=(TICKS,),
            in_specs=[
                pl.BlockSpec((ROWS, MEMBERS), lambda t, w: (0, 0)),
                pl.BlockSpec((1, ROWS, SLOTS), lambda t, w: (t, 0, 0)),
            ]
            + ([four] * 7 + [two] * 2 + [four]) * 2,
            out_specs=pl.BlockSpec((ROWS, MEMBERS), lambda t, w: (0, 0)),
            scratch_shapes=[pltpu.VMEM((OBS, 3 * MEMBERS), BF16), pltpu.VMEM((3 * OBS, MEMBERS), BF16)],
        ),
        cost_estimate=pl.CostEstimate(flops=48 * ROWS * SLOTS * MEMBERS, bytes_accessed=16 << 20, transcendentals=0),
        compiler_params=pltpu.CompilerParams(vmem_limit_bytes=28 << 20),
        name="ticks",
    )(core.reshape(1), state, local, *own, *par)


def on_device(state, taper, block_mask, anom_fly, incr_fly, anom_new, incr_new):
    region, place = lax.axis_index("region"), lax.axis_index("var")
    core, y = region % 2, region // 2
    share = chip_shares(core, y, anom_fly, incr_fly, anom_new, incr_new)
    table = slot_table(core, place // 4, place % 4)

    def make_local(after):
        held_taper, held_mask, held_table, _ = lax.optimization_barrier((taper, block_mask, table, after))
        return localizers(held_taper, held_mask, held_table)

    own, par, local = gather_pieces(core, share, make_local)
    return run_ticks(core, state, local, own, par)


def solution(mesh):
    in_specs = (
        P(("region", "var"), None),
        P(None, ("region", "var"), None),
        P(None, ("region", "var"), None),
        P("region", "var", None),
        P("region", "var", None),
        P(None, "var", None),
        P(None, "var", None),
    )

    return jax.shard_map(on_device, mesh=mesh, in_specs=in_specs, out_specs=P(("region", "var"), None), check_vma=False)
```

```python
import jax
import jax.numpy as jnp
import numpy as np
from jax import lax
from jax.experimental import pallas as pl
from jax.experimental.pallas import tpu as pltpu
from jax.sharding import PartitionSpec as P


MEMBERS = 768
HALF = 384
OBS = 384
BLOCK = 128
TICKS = 4
ROWS = 512
SHARE = 12
PACK = 24
SLOTS = 384
N_VAR = 32
N_Y = 8
F32 = jnp.float32
BF16 = jnp.bfloat16


def route(move):
    pairs = []
    for y in range(N_Y):
        for core in range(2):
            for z in range(8):
                for x in range(4):
                    to = move(y, core, z, x)
                    if to is not None:
                        ty, tc, tz, tx = to
                        here = (y * 2 + core) * N_VAR + z * 4 + x
                        there = (ty * 2 + tc) * N_VAR + (tz % 8) * 4 + tx % 4
                        pairs.append((here, there))
    return pairs


def send(block, move):
    return lax.ppermute(block, ("region", "var"), route(move))


def flip(y, core, z, x):
    return y, 1 - core, z, x


def up_y(step):
    return lambda y, core, z, x: (y + step, core, z, x) if y + step < N_Y else None


def pack_kernel(core_ref, *refs):
    core = core_ref[0]
    mine_ref, other_ref, fresh_ref = refs[4:7]
    copies = [pltpu.make_async_copy(refs[i], refs[7 + i], refs[11].at[i]) for i in range(4)]
    for copy in copies:
        copy.start()
    for copy in copies:
        copy.wait()
    anom_ref, incr_ref, anom_new_ref, incr_new_ref = refs[7:11]
    for col in range(HALF // BLOCK):
        to = slice(col * BLOCK, (col + 1) * BLOCK)
        for half, out_ref in ((core, mine_ref), (1 - core, other_ref)):
            lane = half * (HALF // BLOCK) + col
            anom = anom_ref[pl.ds(lane, SHARE, stride=MEMBERS // BLOCK), :]
            incr = incr_ref[pl.ds(lane, SHARE, stride=MEMBERS // BLOCK), :]
            out_ref[0:8, to], out_ref[8:16, to] = anom[:8], incr[:8]
            out_ref[16:20, to], out_ref[20:24, to] = anom[8:], incr[8:]
    mine = pl.ds(pl.multiple_of(core * HALF, BLOCK), HALF)
    for batch in range(3):
        fresh_ref[batch, 0:8] = anom_new_ref[batch, 0:8, mine]
        fresh_ref[batch, 8:16] = incr_new_ref[batch, 0:8, mine]
        fresh_ref[batch, 16:20] = anom_new_ref[batch, 8:12, mine]
        fresh_ref[batch, 20:24] = incr_new_ref[batch, 8:12, mine]


def chip_shares(core, y, anom_fly, incr_fly, anom_new, incr_new):
    flat = (SHARE * MEMBERS // BLOCK, BLOCK)
    tile = (PACK, HALF)
    vmem = pl.BlockSpec(memory_space=pltpu.VMEM)
    mine, give, fresh = pl.pallas_call(
        pack_kernel,
        out_shape=tuple(jax.ShapeDtypeStruct(o, F32) for o in (tile, tile, (3, *tile))),
        in_specs=[pl.BlockSpec(memory_space=pltpu.SMEM)] + [pl.BlockSpec(memory_space=pltpu.HBM)] * 4,
        out_specs=(vmem, vmem, vmem),
        scratch_shapes=[pltpu.VMEM(flat, F32)] * 2
        + [pltpu.VMEM((3, SHARE, MEMBERS), F32)] * 2
        + [pltpu.SemaphoreType.DMA((4,))],
        compiler_params=pltpu.CompilerParams(vmem_limit_bytes=4 << 20),
        name="pack",
    )(
        core.reshape(1),
        *(pltpu.with_memory_space_constraint(a, pltpu.HBM) for a in (anom_fly.reshape(flat), incr_fly.reshape(flat), anom_new, incr_new)),
    )
    other = send(give, flip)
    pair = jnp.stack([jnp.where(core == 1, mine, other), jnp.where(core == 1, other, mine)])
    below = send(pair, up_y(1))
    below2 = send(pair[0], up_y(2))
    return jnp.stack(
        [
            pair[0],
            pair[1],
            jnp.where(y == 0, fresh[0], below[0]),
            jnp.where(y == 0, fresh[1], below[1]),
            jnp.where(y == 0, fresh[2], jnp.where(y == 1, fresh[0], below2)),
        ]
    )


FAR_Z = (0, 1, -1, 2, -2, 3, -3, 4)
FAR_X = (0, 1, -1, 2)


def piece_order():
    first = [(dz, dx) for dz in (0, 4, 1, -1, 2, -2, 3, -3) for dx in FAR_X]
    second = []
    for dx, part in ((0, 0), (0, 1), (1, 0), (-1, 0), (1, 1), (-1, 1), (2, 0), (2, 1)):
        second += [(dz, dx) for dz in FAR_Z[4 * part : 4 * part + 4]]
    return first, second


ORDER = piece_order()
PARTNER = tuple(tuple(ORDER[1 - core].index(piece) for piece in ORDER[core]) for core in range(2))


def both(to_first, to_second):
    def move(y, core, z, x):
        way = (to_first, to_second)[core]
        return None if way is None else (y, core, z + way[0], x + way[1])

    return move


def gather_pieces(core, share, make_local):
    first = core == 0
    up, down = both((1, 0), (0, 1)), both((-1, 0), (0, -1))
    near_up, near_down = both((0, 1), (1, 0)), both((0, -1), (-1, 0))
    to_second = lambda y, core, z, x: (y, 1, z, x) if core == 0 else None
    to_first = lambda y, core, z, x: (y, 0, z, x) if core == 1 else None
    only_up, only_down = both(None, (1, 0)), both(None, (-1, 0))
    n1 = send(share, near_up)
    n3 = send(share, both((0, 2), (2, 0)))
    n2 = send(share, near_down)
    low = jnp.stack([share, n1, n2, n3])
    up1 = send(low, up)
    down1 = send(low, down)
    n4 = send(n2, only_down)
    n5 = send(n3, only_up)
    n6 = send(n4, only_down)
    n7 = send(n5, only_up)
    high = jnp.stack([n4, n5, n6, n7])
    held = jnp.where(first, up1, high)
    up2 = send(held, up)
    down2 = send(jnp.where(first, down1, high), down)
    par_low = send(low, flip)
    par_up1 = send(up1, flip)
    par_down1 = send(down1, flip)
    local = make_local(held)
    up3 = send(jnp.where(first, up2, up1), up)
    down3 = send(down2, down)
    par_high = send(held, to_first)
    par_up2 = send(up2, flip)
    par_down2 = send(down2, flip)
    far_up = send(up3[:2], both((1, 0), None))
    far_down = send(down3[2:], both((-1, 0), None))
    par_up3 = send(up3, flip)
    par_down3 = send(down3, flip)
    par_far_up = send(far_up, to_second)
    par_far_down = send(far_down, to_second)
    own = [low, up1, down1, up2, down2, up3, down3, far_up, far_down, held]
    par = [par_low, par_up1, par_down1, par_up2, par_down2, par_up3, par_down3, par_far_up, par_far_down, par_high]
    return own, par, local


def slot_table(core, z, x):
    far = jnp.asarray(np.array(ORDER, np.int32))[core]
    source = ((z - far[:, 0]) % 8) * 4 + (x - far[:, 1]) % 4
    lane = jnp.arange(SHARE)
    rows = source[:, None] * SHARE + lane[None, :]
    obs = jnp.concatenate([rows[:, :8].reshape(-1), rows[:, 8:].reshape(-1)])
    return (jnp.arange(OBS)[:, None] == obs[None, :]).astype(BF16)


def localize_kernel(mask_ref, taper_ref, table_ref, out_ref):
    tick = pl.program_id(0)
    for rb in range(ROWS // BLOCK):
        rows = pl.ds(rb * BLOCK, BLOCK)
        parts = []
        for ob in range(OBS // BLOCK):
            flag = mask_ref[(tick * (ROWS // BLOCK) + rb) * (OBS // BLOCK) + ob].astype(F32).astype(BF16)
            tile = taper_ref[0, rows, pl.ds(ob * BLOCK, BLOCK)]
            parts.append(tile * flag)
        kept = jnp.concatenate(parts, axis=1)
        out_ref[0, rows, :] = jnp.dot(kept, table_ref[...], preferred_element_type=F32).astype(BF16)


def localizers(taper, block_mask, table):
    return pl.pallas_call(
        localize_kernel,
        out_shape=jax.ShapeDtypeStruct((TICKS, ROWS, SLOTS), BF16),
        grid_spec=pltpu.PrefetchScalarGridSpec(
            num_scalar_prefetch=1,
            grid=(TICKS,),
            in_specs=[
                pl.BlockSpec((1, ROWS, OBS), lambda t, m: (t, 0, 0)),
                pl.BlockSpec((OBS, SLOTS), lambda t, m: (0, 0)),
            ],
            out_specs=pl.BlockSpec((1, ROWS, SLOTS), lambda t, m: (t, 0, 0)),
        ),
        cost_estimate=pl.CostEstimate(flops=8 * ROWS * OBS * SLOTS, bytes_accessed=4 << 20, transcendentals=0),
        compiler_params=pltpu.CompilerParams(vmem_limit_bytes=8 << 20),
        name="localize",
    )(block_mask.reshape(-1), taper, table)


def halves(a):
    hi = a.astype(BF16)
    return hi, (a - hi.astype(F32)).astype(BF16)


def ticks_kernel(where_ref, state_ref, local_ref, *refs):
    own_refs, par_refs, out_ref, y_rows, d_rows = refs[:10], refs[10:20], refs[20], refs[21], refs[22]
    core = where_ref[0]

    @pl.when(pl.program_id(0) == 0)
    def _():
        out_ref[...] = state_ref[...]

    def piece(held, at, of_first):
        array, part = at // 4, at % 4
        if array == 1 and of_first:
            return held[7 + part // 2][part % 2, 0]
        return held[9 if array == 1 else max(array - 1, 0)][part, 0]

    def put(columns, at, anom, incr):
        hi, lo = halves(anom)
        for part, value in enumerate((hi, lo, hi)):
            y_rows[at : at + 16, part * MEMBERS + columns : part * MEMBERS + columns + HALF] = value
        hi, lo = halves(incr)
        for part, value in enumerate((hi, lo, hi)):
            d_rows[part * OBS + at : part * OBS + at + 16, columns : columns + HALF] = value

    upper = lax.broadcasted_iota(jnp.int32, (8, HALF), 0) < 4

    def arrange(rows, pieces):
        for at in range(0, N_VAR, 4):
            four = pieces(at)
            for k in (0, 2):
                pair = four[k : k + 2]
                put(
                    rows,
                    8 * (at + k),
                    jnp.concatenate([p[0:8] for p in pair], axis=0),
                    jnp.concatenate([p[8:16] for p in pair], axis=0),
                )
            rest = [p[16:24] for p in four]
            turned = [pltpu.roll(p, 4, 0) for p in rest]
            put(
                rows,
                256 + 4 * at,
                jnp.concatenate([jnp.where(upper, rest[k], turned[k + 1]) for k in (0, 2)], axis=0),
                jnp.concatenate([jnp.where(upper, turned[k], rest[k + 1]) for k in (0, 2)], axis=0),
            )

    for me in range(2):

        @pl.when(core == me)
        def _(me=me):
            arrange(me * HALF, lambda at: [piece(own_refs, at + k, me == 0) for k in range(4)])
            arrange((1 - me) * HALF, lambda at: [piece(par_refs, PARTNER[me][at + k], me == 1) for k in range(4)])

    def product(a, b, dims):
        hi, lo = halves(a)
        return lax.dot_general(
            jnp.concatenate([hi, hi, lo], axis=1), b[...], (dims, ((), ())), preferred_element_type=F32
        )

    cross = product(out_ref[...], y_rows, ((1,), (1,)))
    weight = local_ref[0].astype(F32) * cross * (1.0 / (MEMBERS - 1))
    out_ref[...] += product(weight, d_rows, ((1,), (0,)))


def run_ticks(core, state, local, own, par):
    four, two = (
        pl.BlockSpec((n, 1, PACK, HALF), lambda t, w: (0, 1 - w[0] + t, 0, 0)) for n in (4, 2)
    )
    return pl.pallas_call(
        ticks_kernel,
        out_shape=jax.ShapeDtypeStruct((ROWS, MEMBERS), F32),
        grid_spec=pltpu.PrefetchScalarGridSpec(
            num_scalar_prefetch=1,
            grid=(TICKS,),
            in_specs=[
                pl.BlockSpec((ROWS, MEMBERS), lambda t, w: (0, 0)),
                pl.BlockSpec((1, ROWS, SLOTS), lambda t, w: (t, 0, 0)),
            ]
            + ([four] * 7 + [two] * 2 + [four]) * 2,
            out_specs=pl.BlockSpec((ROWS, MEMBERS), lambda t, w: (0, 0)),
            scratch_shapes=[pltpu.VMEM((OBS, 3 * MEMBERS), BF16), pltpu.VMEM((3 * OBS, MEMBERS), BF16)],
        ),
        cost_estimate=pl.CostEstimate(flops=48 * ROWS * SLOTS * MEMBERS, bytes_accessed=16 << 20, transcendentals=0),
        compiler_params=pltpu.CompilerParams(vmem_limit_bytes=22 << 20),
        name="ticks",
    )(core.reshape(1), state, local, *own, *par)


def on_device(state, taper, block_mask, anom_fly, incr_fly, anom_new, incr_new):
    region, place = lax.axis_index("region"), lax.axis_index("var")
    core, y = region % 2, region // 2
    share = chip_shares(core, y, anom_fly, incr_fly, anom_new, incr_new)
    table = slot_table(core, place // 4, place % 4)

    def make_local(after):
        held_taper, held_mask, held_table, _ = lax.optimization_barrier((taper, block_mask, table, after))
        return localizers(held_taper, held_mask, held_table)

    own, par, local = gather_pieces(core, share, make_local)
    return run_ticks(core, state, local, own, par)


def solution(mesh):
    in_specs = (
        P(("region", "var"), None),
        P(None, ("region", "var"), None),
        P(None, ("region", "var"), None),
        P("region", "var", None),
        P("region", "var", None),
        P(None, "var", None),
        P(None, "var", None),
    )

    return jax.shard_map(on_device, mesh=mesh, in_specs=in_specs, out_specs=P(("region", "var"), None), check_vma=False)
```
